32 devices in a mesh: shard: 8 (over y, x, core), rep: 4 (over z).
Axes of the slice: x: 2, y: 2, z: 4, core: 2. Of those that a mesh axis runs over, the one named last changes fastest.
Arguments:
- pooled_grad: float32 [128, 4, 8, 256], P('shard', 'rep'), may hold values from -0.8 to 0.8
- bag_lengths: int32 [8, 4, 128], P('shard', 'rep'), may hold values from 1 to 64, 2048 in all within a row
- row_slots: int32 [8, 4, 2048], P('shard', 'rep'), may hold values from 0 to 511
- id_weights: int32 [8, 4, 2048], P('shard', 'rep'), may hold values from 1 to 32
- touched_rows: float32 [8, 512, 256], P('shard'), may hold values from -6 to 6
- accumulator: float32 [8, 512], P('shard'), may hold values from 0.005 to 0.5
Outputs:
- row_grad: float32 [8, 512, 256], P('shard', 'rep')
- updated_rows: float32 [8, 512, 256], P('shard')
The draws below stay inside these ranges and needn't reach their ends.
Inputs may be any that keep to these rules, and one draw needn't show every extreme that they name: `bag_lengths`: in each table and replica group the bag lengths sum to 2048.
All inputs are finite; a program needn't handle non-finite values.
Results may differ from the reference program's by a relative error of at most 0.0003.
Values sent between devices are 32-bit elements; how exact they have to be, the bound alone decides.
A program may use at most 64 MiB of HBM per device.

```python
import math
import jax
import jax.numpy as jnp
import numpy as np
from jax import lax

E = 256
MOST = 64
SLOTS = 512
TABLES = 8
REPS = 4
SH_SAMPLES = 128
ENTRIES = 2048


def with_ends(result, own_key, low, top_value):
    longest = result.shape.index(max(result.shape))
    spots = []
    for shift in (0, 1):
        where = [jax.random.randint(jax.random.fold_in(own_key, axis), (), 0, length) for axis, length in enumerate(result.shape)]
        where[longest] = (where[longest] + shift) % result.shape[longest]
        spots.append(tuple(where))
    return result.at[spots[0]].set(low).at[spots[1]].set(top_value)


def level_of(rng, extent, cuts, smallest, top_value):
    factor_of, own = 1.0, jax.random.fold_in(rng, 6)
    for dim, parts in cuts:
        heights = jnp.exp(jax.random.uniform(jax.random.fold_in(own, dim), (parts,), jnp.float32, smallest / len(cuts), top_value / len(cuts)))
        factor_of = factor_of * jnp.repeat(heights, extent[dim] // parts).reshape([-1 if axis == dim else 1 for axis in range(len(extent))])
    return factor_of


def rank_table(count, slope):
    portions = [(1 << 20) // math.isqrt(rank ** slope) + 1 for rank in range(1, count + 1)]
    scale = 1 + sum(portions) // (1 << 30)
    return np.cumsum(np.array([max(1, weight // scale) for weight in portions]))


def ranked(stream_key, dims, amount, lean):
    table = rank_table(amount, lean)
    pick = jax.random.randint(jax.random.fold_in(stream_key, 1), dims, 0, int(table[amount - 1]))
    grade = jnp.searchsorted(jnp.asarray(table, jnp.int32), pick, side="right")
    return jax.random.permutation(jax.random.fold_in(stream_key, 2), amount)[grade].astype(jnp.int32)


def length_profile(count, total, reach, skew):
    loads = [(1 << 20) // math.isqrt(standing ** skew) + 1 for standing in range(2, count + 1)]
    surplus, holding = total - reach - (count - 1), [1] * (count - 1)
    while surplus > 0:
        movable = [i for i in range(count - 1) if holding[i] < reach]
        mass, remaining = sum([loads[i] for i in movable]), surplus
        for i in movable:
            more = min(reach - holding[i], max(1, remaining * loads[i] // mass), surplus)
            holding[i] = holding[i] + more
            surplus = surplus - more
    return np.array([reach] + holding)


def uneven_parts(rng, number_of, total, bound, slope):
    if number_of == 2:
        one = jax.random.randint(rng, (), max(1, total - bound), min(bound, total - 1) + 1)
        return jnp.stack([one, total - one])
    sizes = jnp.asarray(length_profile(number_of, total, bound, slope), jnp.int32)
    pairs = (number_of - 1) // 2
    giver, sink = sizes[1:1 + 2 * pairs:2], sizes[2:2 + 2 * pairs:2]
    slack = jnp.minimum(giver - 1, bound - sink)
    moved = jax.random.randint(jax.random.fold_in(rng, 1), (pairs,), 0, 1 << 20) % (slack + 1)
    sizes = sizes.at[1:1 + 2 * pairs:2].set(giver - moved).at[2:2 + 2 * pairs:2].set(sink + moved)
    return sizes[jax.random.permutation(jax.random.fold_in(rng, 2), number_of)]


def scatter_about(key, extent, spread, limit, cuts=(), kind=jnp.bfloat16):
    result = spread * jax.random.normal(key, extent, jnp.float32)
    if cuts:
        result = result * level_of(key, extent, cuts, -0.22, 0.18)
    return jnp.clip(result, -limit, limit).astype(kind)


def setup_inputs(seed: int = 0) -> dict:
    key_of = jax.random.split(jax.random.key(seed), 7)
    pooled_grad = scatter_about(key_of[0], (SH_SAMPLES, REPS, TABLES, E), 0.1, 0.8, ((0, 8), (1, 4)), jnp.float32)
    bag_lengths = jax.vmap(lambda own: uneven_parts(own, SH_SAMPLES, ENTRIES, MOST, 2))(jax.random.split(key_of[1], TABLES * REPS)).reshape((TABLES, REPS, SH_SAMPLES)).astype(jnp.int32)
    row_slots = with_ends(ranked(key_of[2], (TABLES, REPS, ENTRIES), SLOTS, 2), jax.random.fold_in(key_of[2], 3), 0, SLOTS - 1).astype(jnp.int32)
    id_weights = with_ends(jax.random.randint(key_of[3], (TABLES, REPS, ENTRIES), 1, 33), jax.random.fold_in(key_of[3], 1), 1, 32).astype(jnp.int32)
    touched_rows = scatter_about(key_of[4], (TABLES, SLOTS, E), 1.0, 6.0, ((0, 8),), jnp.float32)
    accumulator = jnp.clip(jnp.exp(math.log(0.5) - 4.6051702 * jax.random.uniform(key_of[5], (TABLES, SLOTS), jnp.float32) ** level_of(key_of[5], (TABLES, SLOTS), ((0, 8),), -0.2, 0.2)), 0.005, 0.5)
    return {"pooled_grad": pooled_grad, "bag_lengths": bag_lengths, "row_slots": row_slots, "id_weights": id_weights, "touched_rows": touched_rows, "accumulator": accumulator}


learn_rate = 0.5

def one_table(index, pooled_grad, bag_lengths, row_slots, id_weights):
    total = jnp.zeros((SLOTS, E), jnp.float32)
    positions = jnp.arange(ENTRIES, dtype=jnp.int32)
    for group in range(REPS):
        ends = jnp.cumsum(bag_lengths[index, group]).astype(jnp.int32)
        bags = jnp.searchsorted(ends, positions, side='right').astype(jnp.int32)
        column = pooled_grad[:, group, index]
        scaled = id_weights[index, group].astype(jnp.float32) * 0.0625
        picked = jnp.take(column, bags, axis=0) * scaled[:, None]
        total = total + jax.ops.segment_sum(picked, row_slots[index, group], num_segments=SLOTS)
    return total

def reference(pooled_grad, bag_lengths, row_slots, id_weights, touched_rows, accumulator):
    grads = lax.map(lambda index: one_table(index, pooled_grad, bag_lengths, row_slots, id_weights), jnp.arange(TABLES, dtype=jnp.int32))
    new_state = accumulator + lax.optimization_barrier(jnp.mean(grads * grads, axis=-1))
    updated = touched_rows - learn_rate * grads / (jnp.sqrt(new_state)[..., None] + 1e-08)
    return (grads, updated)
```

```python
import functools

import jax
import jax.numpy as jnp
from jax import lax
from jax.experimental import pallas as pl
from jax.experimental.pallas import tpu as pltpu
from jax.sharding import PartitionSpec as P

learn_rate = 0.5
MESH = pl.DeviceIdType.MESH


def loop(count, body):
    if count <= 8:
        for i in range(count):
            body(i)
    else:

        @pl.loop(0, count)
        def _(i):
            body(i)


def paired(me, i, count):
    if count & (count - 1):
        return lax.rem(me + i, count)
    out, bit = 0, 1
    while bit < count:
        a = (me // bit) % 2
        b = (i // bit) % 2
        out = out + bit * ((a + b) % 2)
        bit *= 2
    return out


def ring_src(me, i, count):
    if count & (count - 1):
        return lax.rem(me - i + count, count)
    return paired(me, i, count)


def kernel(
    shards, reps, chunks,
    pooled, lengths, slots, weights, touched, state,
    grad_out, rows_out,
    pooled_v, staged, samples, slots_v, weights_v, lengths_v, tally_v, acc, touched_v,
    load_sem, a2a_send, a2a_recv, z_send, z_recv, id_send, id_recv,
):
    me, z = lax.axis_index("shard"), lax.axis_index("rep")
    per = staged.shape[1]
    height, width = acc.shape
    count = samples.shape[1]
    entries = slots_v.shape[2]
    group = shards // chunks
    rows = group * per

    load_pooled = pltpu.make_async_copy(pooled, pooled_v, load_sem.at[0])
    load_touched = pltpu.make_async_copy(touched, touched_v, load_sem.at[1])
    load_pooled.start()
    load_touched.start()

    barrier = pltpu.get_barrier_semaphore()

    def greet(i):
        pl.semaphore_signal(
            barrier, inc=1, device_id={"shard": paired(me, i + 1, shards)}, device_id_type=MESH
        )

    @pl.when(z > 0)
    def _():
        pl.semaphore_signal(barrier, inc=1, device_id={"rep": z - 1}, device_id_type=MESH)

    @pl.when(z < reps - 1)
    def _():
        pl.semaphore_signal(barrier, inc=1, device_id={"rep": z + 1}, device_id_type=MESH)

    loop(shards - 1, greet)

    slots_v[z] = slots[0]
    weights_v[z] = weights[0]
    lengths_v[z] = lengths[0]
    load_pooled.wait()

    def stage(t):
        staged[t] = pooled_v[:, 0, t, :]

    loop(shards, stage)
    samples[z, pl.ds(pl.multiple_of(me * per, per), per), :] = staged[me]

    extra = jnp.where(z > 0, 1, 0) + jnp.where(z < reps - 1, 1, 0)
    pl.semaphore_wait(barrier, shards - 1 + extra)

    sides = ((0, 1), (1, -1))

    def id_copies(g, side, step):
        out = []
        for n, (own, buf) in enumerate(
            ((slots, slots_v), (weights, weights_v), (lengths, lengths_v))
        ):
            out.append(
                pltpu.make_async_remote_copy(
                    src_ref=buf.at[g],
                    dst_ref=buf.at[g],
                    send_sem=id_send.at[side, g, n],
                    recv_sem=id_recv.at[g, n],
                    device_id={"rep": z + step},
                    device_id_type=MESH,
                )
            )
        return out

    def chunk_copy(g, c, side, step):
        part = samples.at[g, pl.ds(pl.multiple_of(c * rows, rows), rows), :]
        return pltpu.make_async_remote_copy(
            src_ref=part,
            dst_ref=part,
            send_sem=z_send.at[side, g, c],
            recv_sem=z_recv.at[g, c],
            device_id={"rep": z + step},
            device_id_type=MESH,
        )

    def has_next(step):
        return (z + step >= 0) & (z + step < reps)

    def a2a_copy(peer, src):
        return pltpu.make_async_remote_copy(
            src_ref=staged.at[peer],
            dst_ref=samples.at[z, pl.ds(pl.multiple_of(src * per, per), per), :],
            send_sem=a2a_send.at[peer],
            recv_sem=a2a_recv.at[src],
            device_id={"shard": peer},
            device_id_type=MESH,
        )

    def send_one(i):
        a2a_copy(paired(me, i + 1, shards), me).start()

    for side, step in sides:

        @pl.when(has_next(step))
        def _(side=side, step=step):
            for copy in id_copies(z, side, step):
                copy.start()

    loop(shards - 1, send_one)

    def tally(g, slot):
        span = min(512, entries)
        lens = lengths_v[g].astype(jnp.float32)
        ii = lax.broadcasted_iota(jnp.int32, (count, count), 0)
        jj = lax.broadcasted_iota(jnp.int32, (count, count), 1)
        ends = jnp.sum(jnp.where(jj <= ii, lens, 0.0), axis=1, keepdims=True).astype(jnp.int32)
        starts = jnp.sum(jnp.where(jj < ii, lens, 0.0), axis=1, keepdims=True).astype(jnp.int32)

        def block(b, total):
            at = pl.multiple_of(b * span, span)
            target = slots_v[g, :, pl.ds(at, span)]
            factor = weights_v[g, :, pl.ds(at, span)].astype(jnp.float32)
            pos = at + lax.broadcasted_iota(jnp.int32, (1, span), 1)
            inside = (pos >= starts) & (pos < ends)
            member = jnp.where(inside, 1.0, 0.0).astype(jnp.bfloat16)
            ids = lax.broadcasted_iota(jnp.int32, (height, span), 0)
            chosen = jnp.where(ids == target, factor, 0.0).astype(jnp.bfloat16)
            return total + lax.dot_general(
                chosen, member, (((1,), (1,)), ((), ())), preferred_element_type=jnp.float32
            )

        total = lax.fori_loop(
            0, entries // span, block, jnp.zeros((height, count), jnp.float32)
        )
        high = total.astype(jnp.bfloat16)
        low = (total - high.astype(jnp.float32)).astype(jnp.bfloat16)
        tally_v[slot, :, :count] = high
        tally_v[slot, :, count:] = low

    def add(g, slot, first=False):
        rest = samples[g]
        total = None
        for _ in range(3):
            part = rest.astype(jnp.bfloat16)
            rest = rest - part.astype(jnp.float32)
            term = jnp.dot(
                tally_v[slot],
                jnp.concatenate([part, part], axis=0),
                preferred_element_type=jnp.float32,
            )
            total = term if total is None else total + term
        if first:
            acc[...] = total
        else:
            acc[...] += total

    tally(z, 0)

    def own_chunk(i):
        c = paired(me // group, i, chunks)

        def arrive(q):
            src = c * group + q

            @pl.when(src != me)
            def _():
                a2a_copy(src, src).wait_recv()

        if group == 1:
            if i > 0:
                a2a_copy(c, c).wait_recv()
        else:
            loop(group, arrive)
        for side, step in sides:

            @pl.when(has_next(step))
            def _(side=side, step=step):
                chunk_copy(z, c, side, step).start()

    for i in range(chunks):
        own_chunk(i)

    add(z, 0, first=True)

    for k in range(1, reps):
        for side, step in sides:
            g = z - k * step

            @pl.when((g >= 0) & (g < reps))
            def _(side=side, step=step, g=g):
                for copy in id_copies(g, side, step):
                    copy.wait_recv()
                if k < reps - 1:

                    @pl.when(has_next(step))
                    def _():
                        for copy in id_copies(g, side, step):
                            copy.start()

        @pl.loop(0, 2)
        def _(side):
            g = z - k * (1 - 2 * side)

            @pl.when((g >= 0) & (g < reps))
            def _():
                tally(g, side)

        for i in range(chunks):
            for side, step in sides:
                g = z - k * step

                @pl.when((g >= 0) & (g < reps))
                def _(side=side, step=step, g=g):
                    c = paired(me // group, i, chunks)
                    chunk_copy(g, c, side, step).wait_recv()
                    if k < reps - 1:

                        @pl.when(has_next(step))
                        def _():
                            chunk_copy(g, c, side, step).start()

        @pl.loop(0, 2)
        def _(side):
            g = z - k * (1 - 2 * side)

            @pl.when((g >= 0) & (g < reps))
            def _():
                add(g, side)

    load_touched.wait()
    acc[...] = acc[...] * 0.0625
    part = height // reps
    grad_out[0] = acc[pl.ds(pl.multiple_of(z * part, part), part), :]
    block = min(128, height)
    ii = lax.broadcasted_iota(jnp.int32, (block, block), 0)
    jj = lax.broadcasted_iota(jnp.int32, (block, block), 1)
    for b in range(height // block):
        at = slice(b * block, (b + 1) * block)
        grads = acc[at, :]
        old = jnp.sum(jnp.where(ii == jj, state[:, at], 0.0), axis=1, keepdims=True)
        new = old + jnp.sum(grads * grads, axis=1, keepdims=True) * (1.0 / width)
        rows_out[0, at, :] = touched_v[0, at, :] - grads * (learn_rate / (jnp.sqrt(new) + 1e-08))

    def sent(i):
        peer = paired(me, i + 1, shards)
        a2a_copy(peer, me).wait_send()

    loop(shards - 1, sent)
    for k in range(reps - 1):
        for side, step in sides:
            g = z - k * step

            @pl.when((g >= 0) & (g < reps) & has_next(step))
            def _(side=side, step=step, g=g):
                for copy in id_copies(g, side, step):
                    copy.wait_send()
                for c in range(chunks):
                    chunk_copy(g, c, side, step).wait_send()


def per_device(pooled_grad, bag_lengths, row_slots, id_weights, touched_rows, accumulator):
    shards, reps = lax.axis_size("shard"), lax.axis_size("rep")
    per, _, tables, width = pooled_grad.shape
    height = touched_rows.shape[1]
    entries = row_slots.shape[2]
    count = per * shards
    chunks = min(8, shards)
    vmem = pl.BlockSpec(memory_space=pltpu.VMEM)
    hbm = pl.BlockSpec(memory_space=pl.ANY)
    dma = pltpu.SemaphoreType.DMA
    return pl.pallas_call(
        functools.partial(kernel, shards, reps, chunks),
        out_shape=(
            jax.ShapeDtypeStruct((1, height // reps, width), jnp.float32),
            jax.ShapeDtypeStruct((1, height, width), jnp.float32),
        ),
        in_specs=[hbm, vmem, vmem, vmem, hbm, vmem],
        out_specs=(vmem, vmem),
        scratch_shapes=[
            pltpu.VMEM((per, 1, tables, width), jnp.float32),
            pltpu.VMEM((tables, per, width), jnp.float32),
            pltpu.VMEM((reps, count, width), jnp.float32),
            pltpu.VMEM((reps, 1, entries), jnp.int32),
            pltpu.VMEM((reps, 1, entries), jnp.int32),
            pltpu.VMEM((reps, 1, count), jnp.int32),
            pltpu.VMEM((2, height, 2 * count), jnp.bfloat16),
            pltpu.VMEM((height, width), jnp.float32),
            pltpu.VMEM((1, height, width), jnp.float32),
            dma((2,)),
            dma((shards,)),
            dma((shards,)),
            dma((2, reps, chunks)),
            dma((reps, chunks)),
            dma((2, reps, 3)),
            dma((reps, 3)),
        ],
        compiler_params=pltpu.CompilerParams(
            collective_id=0, has_side_effects=True, vmem_limit_bytes=60 * 1024 * 1024
        ),
    )(pooled_grad, bag_lengths, row_slots, id_weights, touched_rows, accumulator)


def solution(mesh):
    placed = (
        P("shard", "rep", None, None),
        P("shard", "rep", None),
        P("shard", "rep", None),
        P("shard", "rep", None),
        P("shard", None, None),
        P("shard", None),
    )
    return jax.shard_map(
        per_device,
        mesh=mesh,
        in_specs=placed,
        out_specs=(P("shard", "rep", None), P("shard", None, None)),
        check_vma=False,
    )
```

```python
import functools

import jax
import jax.numpy as jnp
from jax import lax
from jax.experimental import pallas as pl
from jax.experimental.pallas import tpu as pltpu
from jax.sharding import PartitionSpec as P

learn_rate = 0.5
CHUNKS = 4
REACH = 1
MESH = pl.DeviceIdType.MESH


def loop(count, body):
    if count <= 8:
        for i in range(count):
            body(i)
    else:

        @pl.loop(0, count)
        def _(i):
            body(i)


def paired(me, i, count):
    if count & (count - 1):
        return lax.rem(me + i, count)
    out, bit = 0, 1
    while bit < count:
        a = (me // bit) % 2
        b = (i // bit) % 2
        out = out + bit * ((a + b) % 2)
        bit *= 2
    return out


def ring_src(me, i, count):
    if count & (count - 1):
        return lax.rem(me - i + count, count)
    return paired(me, i, count)


def kernel(
    shards, reps, chunks, reach,
    pooled, lengths, slots, weights,
    acc,
    pooled_v, staged, samples, slots_v, weights_v, lengths_v, tally_v,
    load_sem, a2a_send, a2a_recv, z_send, z_recv, id_send, id_recv,
):
    me, z = lax.axis_index("shard"), lax.axis_index("rep")
    per = staged.shape[1]
    height, width = acc.shape
    count = samples.shape[1]
    entries = slots_v.shape[2]
    group = shards // chunks
    rows = group * per

    load_pooled = pltpu.make_async_copy(pooled, pooled_v, load_sem.at[0])
    load_ids = [
        pltpu.make_async_copy(own.at[0], buf.at[z], load_sem.at[1 + n])
        for n, (own, buf) in enumerate(
            ((slots, slots_v), (weights, weights_v), (lengths, lengths_v))
        )
    ]
    load_pooled.start()
    for copy in load_ids:
        copy.start()

    barrier = pltpu.get_barrier_semaphore()

    def greet(i):
        pl.semaphore_signal(
            barrier, inc=1, device_id={"shard": paired(me, i + 1, shards)}, device_id_type=MESH
        )

    for i in range(1, reps):
        pl.semaphore_signal(
            barrier, inc=1, device_id={"rep": lax.rem(z + i, reps)}, device_id_type=MESH
        )
    loop(shards - 1, greet)

    load_pooled.wait()

    def stage(t):
        staged[t] = pooled_v[:, 0, t, :]

    loop(shards, stage)
    samples[z, pl.ds(pl.multiple_of(me * per, per), per), :] = staged[me]

    pl.semaphore_wait(barrier, shards + reps - 2)

    sides = ((0, 1), (1, -1))

    def id_copies(g, peer):
        out = []
        for n, (own, buf) in enumerate(
            ((slots, slots_v), (weights, weights_v), (lengths, lengths_v))
        ):
            out.append(
                pltpu.make_async_remote_copy(
                    src_ref=own.at[0],
                    dst_ref=buf.at[g],
                    send_sem=id_send.at[peer, n],
                    recv_sem=id_recv.at[g, n],
                    device_id={"rep": peer},
                    device_id_type=MESH,
                )
            )
        return out

    def chunk_copy(g, c, peer):
        part = samples.at[g, pl.ds(pl.multiple_of(c * rows, rows), rows), :]
        return pltpu.make_async_remote_copy(
            src_ref=part,
            dst_ref=part,
            send_sem=z_send.at[peer, g, c],
            recv_sem=z_recv.at[g, c],
            device_id={"rep": peer},
            device_id_type=MESH,
        )

    def inside(at):
        return (at >= 0) & (at < reps)

    def a2a_copy(peer, src):
        return pltpu.make_async_remote_copy(
            src_ref=staged.at[peer],
            dst_ref=samples.at[z, pl.ds(pl.multiple_of(src * per, per), per), :],
            send_sem=a2a_send.at[peer],
            recv_sem=a2a_recv.at[src],
            device_id={"shard": peer},
            device_id_type=MESH,
        )

    def send_one(i):
        a2a_copy(paired(me, i + 1, shards), me).start()

    for i in range(1, reps):
        for copy in id_copies(z, lax.rem(z + i, reps)):
            copy.start()

    loop(shards - 1, send_one)

    def tally(g, slot):
        span = min(512, entries)
        lens = lengths_v[g].astype(jnp.float32)
        ii = lax.broadcasted_iota(jnp.int32, (count, count), 0)
        jj = lax.broadcasted_iota(jnp.int32, (count, count), 1)
        ends = jnp.sum(jnp.where(jj <= ii, lens, 0.0), axis=1, keepdims=True).astype(jnp.int32)
        starts = jnp.sum(jnp.where(jj < ii, lens, 0.0), axis=1, keepdims=True).astype(jnp.int32)

        def block(b, total):
            at = pl.multiple_of(b * span, span)
            target = slots_v[g, :, pl.ds(at, span)]
            factor = weights_v[g, :, pl.ds(at, span)].astype(jnp.float32)
            pos = at + lax.broadcasted_iota(jnp.int32, (1, span), 1)
            within = (pos >= starts) & (pos < ends)
            member = jnp.where(within, 1.0, 0.0).astype(jnp.bfloat16)
            ids = lax.broadcasted_iota(jnp.int32, (height, span), 0)
            chosen = jnp.where(ids == target, factor, 0.0).astype(jnp.bfloat16)
            return total + lax.dot_general(
                chosen, member, (((1,), (1,)), ((), ())), preferred_element_type=jnp.float32
            )

        total = lax.fori_loop(
            0, entries // span, block, jnp.zeros((height, count), jnp.float32)
        )
        high = total.astype(jnp.bfloat16)
        low = (total - high.astype(jnp.float32)).astype(jnp.bfloat16)
        tally_v[slot, :, :count] = high
        tally_v[slot, :, count:] = low

    def add(g, slot, first=False):
        rest = samples[g]
        total = None
        for _ in range(3):
            part = rest.astype(jnp.bfloat16)
            rest = rest - part.astype(jnp.float32)
            term = jnp.dot(
                tally_v[slot],
                jnp.concatenate([part, part], axis=0),
                preferred_element_type=jnp.float32,
            )
            total = term if total is None else total + term
        if first:
            acc[...] = total
        else:
            acc[...] += total

    for copy in load_ids:
        copy.wait()
    tally(z, 0)

    def own_chunk(i):
        c = paired(me // group, i, chunks)

        def arrive(q):
            src = c * group + q

            @pl.when(src != me)
            def _():
                a2a_copy(src, src).wait_recv()

        if group == 1:
            if i > 0:
                a2a_copy(c, c).wait_recv()
        else:
            loop(group, arrive)
        for far in range(1, min(reach, reps - 1) + 1):
            for side, step in sides:
                peer = z + far * step

                @pl.when(inside(peer))
                def _(peer=peer):
                    chunk_copy(z, c, peer).start()

    for i in range(chunks):
        own_chunk(i)

    add(z, 0, first=True)

    for k in range(1, reps):
        for side, step in sides:
            g = z - k * step

            @pl.when(inside(g))
            def _(g=g):
                for copy in id_copies(g, g):
                    copy.wait_recv()

        @pl.loop(0, 2)
        def _(side):
            g = z - k * (1 - 2 * side)

            @pl.when((g >= 0) & (g < reps))
            def _():
                tally(g, side)

        for i in range(chunks):
            for side, step in sides:
                g = z - k * step

                @pl.when(inside(g))
                def _(step=step, g=g):
                    c = paired(me // group, i, chunks)
                    chunk_copy(g, c, g).wait_recv()
                    if reach <= k < reps - 1:

                        @pl.when(inside(z + step))
                        def _():
                            chunk_copy(g, c, z + step).start()

        @pl.loop(0, 2)
        def _(side):
            g = z - k * (1 - 2 * side)

            @pl.when((g >= 0) & (g < reps))
            def _():
                add(g, side)

    acc[...] = acc[...] * 0.0625

    def sent(i):
        peer = paired(me, i + 1, shards)
        a2a_copy(peer, me).wait_send()

    loop(shards - 1, sent)
    for i in range(1, reps):
        for copy in id_copies(z, lax.rem(z + i, reps)):
            copy.wait_send()
    for side, step in sides:
        for far in range(1, min(reach, reps - 1) + 1):
            peer = z + far * step

            @pl.when(inside(peer))
            def _(peer=peer):
                for c in range(chunks):
                    chunk_copy(z, c, peer).wait_send()

        for k in range(reach, reps - 1):
            g = z - k * step

            @pl.when(inside(g) & inside(z + step))
            def _(step=step, g=g):
                for c in range(chunks):
                    chunk_copy(g, c, z + step).wait_send()


def finish(reps, acc, touched, state, grad_out, rows_out):
    z = lax.axis_index("rep")
    height, width = acc.shape
    part = height // reps
    grad_out[0] = acc[pl.ds(pl.multiple_of(z * part, part), part), :]
    block = min(128, height)
    ii = lax.broadcasted_iota(jnp.int32, (block, block), 0)
    jj = lax.broadcasted_iota(jnp.int32, (block, block), 1)
    for b in range(height // block):
        at = slice(b * block, (b + 1) * block)
        grads = acc[at, :]
        old = jnp.sum(jnp.where(ii == jj, state[:, at], 0.0), axis=1, keepdims=True)
        new = old + jnp.sum(grads * grads, axis=1, keepdims=True) * (1.0 / width)
        rows_out[0, at, :] = touched[0, at, :] - grads * (learn_rate / (jnp.sqrt(new) + 1e-08))


def per_device(pooled_grad, bag_lengths, row_slots, id_weights, touched_rows, accumulator):
    shards, reps = lax.axis_size("shard"), lax.axis_size("rep")
    per, _, tables, width = pooled_grad.shape
    height = touched_rows.shape[1]
    entries = row_slots.shape[2]
    count = per * shards
    chunks = min(CHUNKS, shards)
    vmem = pl.BlockSpec(memory_space=pltpu.VMEM)
    hbm = pl.BlockSpec(memory_space=pltpu.HBM)
    dma = pltpu.SemaphoreType.DMA
    sent = [
        pltpu.with_memory_space_constraint(x, pltpu.HBM)
        for x in (pooled_grad, bag_lengths, row_slots, id_weights)
    ]
    total = pl.pallas_call(
        functools.partial(kernel, shards, reps, chunks, REACH),
        out_shape=jax.ShapeDtypeStruct((height, width), jnp.float32),
        in_specs=[hbm] * 4,
        out_specs=vmem,
        scratch_shapes=[
            pltpu.VMEM((per, 1, tables, width), jnp.float32),
            pltpu.VMEM((tables, per, width), jnp.float32),
            pltpu.VMEM((reps, count, width), jnp.float32),
            pltpu.VMEM((reps, 1, entries), jnp.int32),
            pltpu.VMEM((reps, 1, entries), jnp.int32),
            pltpu.VMEM((reps, 1, count), jnp.int32),
            pltpu.VMEM((2, height, 2 * count), jnp.bfloat16),
            dma((4,)),
            dma((shards,)),
            dma((shards,)),
            dma((reps, reps, chunks)),
            dma((reps, chunks)),
            dma((reps, 3)),
            dma((reps, 3)),
        ],
        compiler_params=pltpu.CompilerParams(
            collective_id=0, has_side_effects=True, vmem_limit_bytes=40 * 1024 * 1024
        ),
    )(*sent)
    return pl.pallas_call(
        functools.partial(finish, reps),
        out_shape=(
            jax.ShapeDtypeStruct((1, height // reps, width), jnp.float32),
            jax.ShapeDtypeStruct((1, height, width), jnp.float32),
        ),
        in_specs=[vmem] * 3,
        out_specs=(vmem, vmem),
        compiler_params=pltpu.CompilerParams(vmem_limit_bytes=16 * 1024 * 1024),
    )(total, touched_rows, accumulator)


def solution(mesh):
    placed = (
        P("shard", "rep", None, None),
        P("shard", "rep", None),
        P("shard", "rep", None),
        P("shard", "rep", None),
        P("shard", None, None),
        P("shard", None),
    )
    return jax.shard_map(
        per_device,
        mesh=mesh,
        in_specs=placed,
        out_specs=(P("shard", "rep", None), P("shard", None, None)),
        check_vma=False,
    )
```

```python
import functools

import jax
import jax.numpy as jnp
from jax import lax
from jax.experimental import pallas as pl
from jax.experimental.pallas import tpu as pltpu
from jax.sharding import PartitionSpec as P

learn_rate = 0.5
CHUNKS = 4
REACH = 1
MESH = pl.DeviceIdType.MESH


def loop(count, body):
    if count <= 8:
        for i in range(count):
            body(i)
    else:

        @pl.loop(0, count)
        def _(i):
            body(i)


def paired(me, i, count):
    if count & (count - 1):
        return lax.rem(me + i, count)
    out, bit = 0, 1
    while bit < count:
        a = (me // bit) % 2
        b = (i // bit) % 2
        out = out + bit * ((a + b) % 2)
        bit *= 2
    return out


def ring_src(me, i, count):
    if count & (count - 1):
        return lax.rem(me - i + count, count)
    return paired(me, i, count)


def kernel(
    shards, reps, chunks, reach,
    pooled, lengths, slots, weights,
    acc,
    pooled_v, staged, samples, slots_v, weights_v, lengths_v, tally_v,
    load_sem, a2a_send, a2a_recv, z_send, z_recv, id_send, id_recv,
):
    me, z = lax.axis_index("shard"), lax.axis_index("rep")
    per = staged.shape[1]
    height, width = acc.shape
    count = samples.shape[1]
    entries = slots_v.shape[2]
    group = shards // chunks
    rows = group * per

    load_pooled = pltpu.make_async_copy(pooled, pooled_v, load_sem.at[0])
    load_ids = [
        pltpu.make_async_copy(own.at[0], buf.at[z], load_sem.at[1 + n])
        for n, (own, buf) in enumerate(
            ((slots, slots_v), (weights, weights_v), (lengths, lengths_v))
        )
    ]
    load_pooled.start()
    for copy in load_ids:
        copy.start()

    barrier = pltpu.get_barrier_semaphore()

    def greet(i):
        pl.semaphore_signal(
            barrier, inc=1, device_id={"shard": paired(me, i + 1, shards)}, device_id_type=MESH
        )

    for i in range(1, reps):
        pl.semaphore_signal(
            barrier, inc=1, device_id={"rep": lax.rem(z + i, reps)}, device_id_type=MESH
        )
    loop(shards - 1, greet)

    load_pooled.wait()

    def stage(t):
        staged[t] = pooled_v[:, 0, t, :]

    loop(shards, stage)
    samples[z, pl.ds(pl.multiple_of(me * per, per), per), :] = staged[me]

    pl.semaphore_wait(barrier, shards + reps - 2)

    sides = ((0, 1), (1, -1))

    def id_copies(g, peer):
        out = []
        for n, (own, buf) in enumerate(
            ((slots, slots_v), (weights, weights_v), (lengths, lengths_v))
        ):
            out.append(
                pltpu.make_async_remote_copy(
                    src_ref=own.at[0],
                    dst_ref=buf.at[g],
                    send_sem=id_send.at[peer, n],
                    recv_sem=id_recv.at[g, n],
                    device_id={"rep": peer},
                    device_id_type=MESH,
                )
            )
        return out

    def chunk_copy(g, c, peer):
        part = samples.at[g, pl.ds(pl.multiple_of(c * rows, rows), rows), :]
        return pltpu.make_async_remote_copy(
            src_ref=part,
            dst_ref=part,
            send_sem=z_send.at[peer, g, c],
            recv_sem=z_recv.at[g, c],
            device_id={"rep": peer},
            device_id_type=MESH,
        )

    def inside(at):
        return (at >= 0) & (at < reps)

    def a2a_copy(peer, src):
        return pltpu.make_async_remote_copy(
            src_ref=staged.at[peer],
            dst_ref=samples.at[z, pl.ds(pl.multiple_of(src * per, per), per), :],
            send_sem=a2a_send.at[peer],
            recv_sem=a2a_recv.at[src],
            device_id={"shard": peer},
            device_id_type=MESH,
        )

    def send_one(i):
        a2a_copy(paired(me, i + 1, shards), me).start()

    for i in range(1, reps):
        for copy in id_copies(z, lax.rem(z + i, reps)):
            copy.start()

    loop(shards - 1, send_one)

    def tally(g, slot):
        span = min(512, entries)
        lens = lengths_v[g].astype(jnp.float32)
        ii = lax.broadcasted_iota(jnp.int32, (count, count), 0)
        jj = lax.broadcasted_iota(jnp.int32, (count, count), 1)
        ends = jnp.sum(jnp.where(jj <= ii, lens, 0.0), axis=1, keepdims=True).astype(jnp.int32)
        starts = jnp.sum(jnp.where(jj < ii, lens, 0.0), axis=1, keepdims=True).astype(jnp.int32)

        def block(b, total):
            at = pl.multiple_of(b * span, span)
            target = slots_v[g, :, pl.ds(at, span)]
            factor = weights_v[g, :, pl.ds(at, span)].astype(jnp.float32)
            pos = at + lax.broadcasted_iota(jnp.int32, (1, span), 1)
            within = (pos >= starts) & (pos < ends)
            member = jnp.where(within, 1.0, 0.0).astype(jnp.bfloat16)
            ids = lax.broadcasted_iota(jnp.int32, (height, span), 0)
            chosen = jnp.where(ids == target, factor, 0.0).astype(jnp.bfloat16)
            return total + lax.dot_general(
                chosen, member, (((1,), (1,)), ((), ())), preferred_element_type=jnp.float32
            )

        total = lax.fori_loop(
            0, entries // span, block, jnp.zeros((height, count), jnp.float32)
        )
        high = total.astype(jnp.bfloat16)
        low = (total - high.astype(jnp.float32)).astype(jnp.bfloat16)
        tally_v[slot, :, :count] = high
        tally_v[slot, :, count:] = low

    def add(g, slot, first=False):
        rest = samples[g]
        total = None
        for _ in range(3):
            part = rest.astype(jnp.bfloat16)
            rest = rest - part.astype(jnp.float32)
            term = jnp.dot(
                tally_v[slot],
                jnp.concatenate([part, part], axis=0),
                preferred_element_type=jnp.float32,
            )
            total = term if total is None else total + term
        if first:
            acc[...] = total
        else:
            acc[...] += total

    for copy in load_ids:
        copy.wait()
    tally(z, 2)

    def own_chunk(i):
        c = paired(me // group, i, chunks)

        def arrive(q):
            src = c * group + q

            @pl.when(src != me)
            def _():
                a2a_copy(src, src).wait_recv()

        if group == 1:
            if i > 0:
                a2a_copy(c, c).wait_recv()
        else:
            loop(group, arrive)
        for far in range(1, min(reach, reps - 1) + 1):
            for side, step in sides:
                peer = z + far * step

                @pl.when(inside(peer))
                def _(peer=peer):
                    chunk_copy(z, c, peer).start()

    for i in range(chunks):
        own_chunk(i)

    for k in range(1, reps):
        for side, step in sides:
            g = z - k * step

            @pl.when(inside(g))
            def _(g=g):
                for copy in id_copies(g, g):
                    copy.wait_recv()

        @pl.loop(0, 2)
        def _(side):
            g = z - k * (1 - 2 * side)

            @pl.when((g >= 0) & (g < reps))
            def _():
                tally(g, side)

        for i in range(chunks):
            for side, step in sides:
                g = z - k * step

                @pl.when(inside(g))
                def _(step=step, g=g):
                    c = paired(me // group, i, chunks)
                    chunk_copy(g, c, g).wait_recv()
                    if reach <= k < reps - 1:

                        @pl.when(inside(z + step))
                        def _():
                            chunk_copy(g, c, z + step).start()

        if k == 1:
            add(z, 2, first=True)

        @pl.loop(0, 2)
        def _(side):
            g = z - k * (1 - 2 * side)

            @pl.when((g >= 0) & (g < reps))
            def _():
                add(g, side)

    acc[...] = acc[...] * 0.0625

    def sent(i):
        peer = paired(me, i + 1, shards)
        a2a_copy(peer, me).wait_send()

    loop(shards - 1, sent)
    for i in range(1, reps):
        for copy in id_copies(z, lax.rem(z + i, reps)):
            copy.wait_send()
    for side, step in sides:
        for far in range(1, min(reach, reps - 1) + 1):
            peer = z + far * step

            @pl.when(inside(peer))
            def _(peer=peer):
                for c in range(chunks):
                    chunk_copy(z, c, peer).wait_send()

        for k in range(reach, reps - 1):
            g = z - k * step

            @pl.when(inside(g) & inside(z + step))
            def _(step=step, g=g):
                for c in range(chunks):
                    chunk_copy(g, c, z + step).wait_send()


def finish(reps, acc, touched, state, grad_out, rows_out):
    z = lax.axis_index("rep")
    height, width = acc.shape
    part = height // reps
    grad_out[0] = acc[pl.ds(pl.multiple_of(z * part, part), part), :]
    block = min(128, height)
    ii = lax.broadcasted_iota(jnp.int32, (block, block), 0)
    jj = lax.broadcasted_iota(jnp.int32, (block, block), 1)
    for b in range(height // block):
        at = slice(b * block, (b + 1) * block)
        grads = acc[at, :]
        old = jnp.sum(jnp.where(ii == jj, state[:, at], 0.0), axis=1, keepdims=True)
        new = old + jnp.sum(grads * grads, axis=1, keepdims=True) * (1.0 / width)
        rows_out[0, at, :] = touched[0, at, :] - grads * (learn_rate / (jnp.sqrt(new) + 1e-08))


def per_device(pooled_grad, bag_lengths, row_slots, id_weights, touched_rows, accumulator):
    shards, reps = lax.axis_size("shard"), lax.axis_size("rep")
    per, _, tables, width = pooled_grad.shape
    height = touched_rows.shape[1]
    entries = row_slots.shape[2]
    count = per * shards
    chunks = min(CHUNKS, shards)
    vmem = pl.BlockSpec(memory_space=pltpu.VMEM)
    hbm = pl.BlockSpec(memory_space=pltpu.HBM)
    dma = pltpu.SemaphoreType.DMA
    sent = [
        pltpu.with_memory_space_constraint(x, pltpu.HBM)
        for x in (pooled_grad, bag_lengths, row_slots, id_weights)
    ]
    total = pl.pallas_call(
        functools.partial(kernel, shards, reps, chunks, REACH),
        out_shape=jax.ShapeDtypeStruct((height, width), jnp.float32),
        in_specs=[hbm] * 4,
        out_specs=vmem,
        scratch_shapes=[
            pltpu.VMEM((per, 1, tables, width), jnp.float32),
            pltpu.VMEM((tables, per, width), jnp.float32),
            pltpu.VMEM((reps, count, width), jnp.float32),
            pltpu.VMEM((reps, 1, entries), jnp.int32),
            pltpu.VMEM((reps, 1, entries), jnp.int32),
            pltpu.VMEM((reps, 1, count), jnp.int32),
            pltpu.VMEM((3, height, 2 * count), jnp.bfloat16),
            dma((4,)),
            dma((shards,)),
            dma((shards,)),
            dma((reps, reps, chunks)),
            dma((reps, chunks)),
            dma((reps, 3)),
            dma((reps, 3)),
        ],
        compiler_params=pltpu.CompilerParams(
            collective_id=0, has_side_effects=True, vmem_limit_bytes=40 * 1024 * 1024
        ),
    )(*sent)
    return pl.pallas_call(
        functools.partial(finish, reps),
        out_shape=(
            jax.ShapeDtypeStruct((1, height // reps, width), jnp.float32),
            jax.ShapeDtypeStruct((1, height, width), jnp.float32),
        ),
        in_specs=[vmem] * 3,
        out_specs=(vmem, vmem),
        compiler_params=pltpu.CompilerParams(vmem_limit_bytes=16 * 1024 * 1024),
    )(total, touched_rows, accumulator)


def solution(mesh):
    placed = (
        P("shard", "rep", None, None),
        P("shard", "rep", None),
        P("shard", "rep", None),
        P("shard", "rep", None),
        P("shard", None, None),
        P("shard", None),
    )
    return jax.shard_map(
        per_device,
        mesh=mesh,
        in_specs=placed,
        out_specs=(P("shard", "rep", None), P("shard", None, None)),
        check_vma=False,
    )
```
